32 devices in a mesh: seq: 8 (over y, x, core), tp: 4 (over z).
Axes of the slice: x: 2, y: 2, z: 4, core: 2. Of those that a mesh axis runs over, the one named last changes fastest.
Arguments:
- gate_input: bfloat16 [8192, 8192], P('seq', 'tp'), may hold values from -6 to 6
- key_input: bfloat16 [8192, 8192], P('seq', 'tp'), may hold values from -6 to 6
- value_input: bfloat16 [8192, 8192], P('seq', 'tp'), may hold values from -6 to 6
- filter_taps: bfloat16 [512, 2048], P('tp'), as said below
- out_weight: bfloat16 [4096, 8192], P(None, 'tp'), may hold values from -0.0625 to 0.0625
Outputs:
- mixed: bfloat16 [4096, 8192], P('tp', 'seq')
The draws below stay inside these ranges and needn't reach their ends.
Inputs may be any that keep to these rules, and one draw needn't show every extreme that they name: `filter_taps`: one causal filter for each group of 16 consecutive channels, indexed by lag.
All inputs are finite; a program needn't handle non-finite values.
Results may differ from the reference program's by a relative error of at most 0.0095.
Values may be sent and summed in bfloat16 or wider, within the bound.
A program may use at most 192 MiB of HBM per device.

```python
import math
import jax
import jax.numpy as jnp
from jax import lax

D = 8192
OUT = 4096
GROUP_SIZE = 16
KERNEL_COHORTS = 512
KERNEL_SPAN_TAPS = 2048
TOKENS = 8192
N_TP = 4


def draw_filter_taps(key, part):
    forked_seed_pairs = jax.random.split(key, 5)
    quick_share = 0.5
    amplitude = jax.random.truncated_normal(forked_seed_pairs[0], -4.0, 4.0, (KERNEL_COHORTS, KERNEL_SPAN_TAPS), jnp.float32)
    quick_groups = jax.random.bernoulli(forked_seed_pairs[1], quick_share, (KERNEL_COHORTS, 1))
    quick_rate = jnp.exp(jax.random.uniform(forked_seed_pairs[2], (KERNEL_COHORTS, 1), jnp.float32, jnp.log(1.0 / 50.0), jnp.log(1.0 / 30.0)))
    slow_rate = jax.random.uniform(forked_seed_pairs[3], (KERNEL_COHORTS, 1), jnp.float32, 0.2, 0.8) / KERNEL_SPAN_TAPS
    decay_rate = jnp.where(quick_groups, quick_rate, slow_rate)
    delay_offset_number = jnp.arange(KERNEL_SPAN_TAPS, dtype=jnp.float32)[None, :]
    spike_sequence = jax.random.randint(forked_seed_pairs[4], (KERNEL_COHORTS, 3), 1, KERNEL_SPAN_TAPS).astype(jnp.float32)
    fading_profile = jnp.exp(-decay_rate * delay_offset_number)
    fading_profile = fading_profile * jnp.where(delay_offset_number >= spike_sequence[:, 0:1], 0.7, 1.0)
    fading_profile = fading_profile * jnp.where(delay_offset_number >= spike_sequence[:, 1:2], 0.7, 1.0)
    fading_profile = fading_profile * jnp.where(delay_offset_number >= spike_sequence[:, 2:3], 0.7, 1.0)
    normalize_factor = jnp.sqrt(2.0 * decay_rate / (1.0 - jnp.exp(-2.0 * decay_rate * KERNEL_SPAN_TAPS)))
    return (amplitude * fading_profile * normalize_factor).astype(jnp.bfloat16)


def steps_of(stream_key, extent, shards, low, top_value):
    def one(dim, blocks):
        draws = jax.random.uniform(jax.random.fold_in(jax.random.fold_in(stream_key, 6), dim), (blocks,), jnp.float32, low / len(shards), top_value / len(shards))
        return jnp.repeat(jnp.exp(draws), extent[dim] // blocks).reshape((-1,) + (1,) * (len(extent) - dim - 1))

    factor_of = one(*shards[0])
    for cut in shards[1:]:
        factor_of = factor_of * one(*cut)
    return factor_of


def centred(key, shape, scale, most, cuts=(), kind=jnp.bfloat16):
    entries = scale * jax.random.normal(key, shape, jnp.float32)
    if cuts:
        entries = entries * steps_of(key, shape, cuts, -0.22, 0.18)
    return jnp.clip(entries, -most, most).astype(kind)


def setup_inputs(seed: int = 0) -> dict:
    keys = jax.random.split(jax.random.key(seed), 6)
    gate_input = centred(keys[0], (TOKENS, D), 1.0, 6.0, ((0, 8), (1, 4)))
    key_input = centred(keys[1], (TOKENS, D), 1.0, 6.0, ((0, 8), (1, 4)))
    value_input = centred(keys[2], (TOKENS, D), 1.0, 6.0, ((0, 8), (1, 4)))
    filter_taps = draw_filter_taps(jax.random.fold_in(keys[5], 71), 0)
    out_weight = centred(keys[4], (OUT, D), D ** -0.5, 0.0625, ((1, 4),))
    return dict(gate_input=gate_input, key_input=key_input, value_input=value_input, filter_taps=filter_taps, out_weight=out_weight)


def causal_conv(signal, taps):
    length = signal.shape[-1]
    padded = length + taps.shape[-1]
    spectrum = jnp.fft.rfft(signal, n=padded, axis=-1) * jnp.fft.rfft(taps, n=padded, axis=-1)[:, None, :]
    return jnp.fft.irfft(spectrum, n=padded, axis=-1)[..., :length]


def smoothed_samples(operands):
    return causal_conv(operands[0], operands[1])


def reference(gate_input, key_input, value_input, filter_taps, out_weight):
    product = (key_input.astype(jnp.float32) * value_input.astype(jnp.float32)).astype(jnp.bfloat16)
    length = product.shape[0]
    signal = product.astype(jnp.float32).reshape(length, KERNEL_COHORTS, GROUP_SIZE).transpose(1, 2, 0)
    taps = filter_taps.astype(jnp.float32)
    batches = math.gcd(KERNEL_COHORTS, 8)
    conv = lax.map(smoothed_samples, (signal.reshape(batches, KERNEL_COHORTS // batches, GROUP_SIZE, length),
                                taps.reshape(batches, KERNEL_COHORTS // batches, KERNEL_SPAN_TAPS)))
    conv = conv.reshape(KERNEL_COHORTS, GROUP_SIZE, length).transpose(2, 0, 1).reshape(length, D)
    gated = (gate_input.astype(jnp.float32) * conv).astype(jnp.bfloat16)
    share = D // N_TP
    weight_parts = out_weight.reshape(OUT, N_TP, share).transpose(1, 0, 2)
    gated_parts = gated.reshape(length, N_TP, share).transpose(1, 0, 2)

    def accumulate(total, operands):
        partial_value = jnp.dot(operands[0], operands[1].T, preferred_element_type=jnp.float32)
        rounded = lax.optimization_barrier(partial_value.astype(jnp.bfloat16))
        return total + rounded.astype(jnp.float32), None

    total = lax.scan(accumulate, jnp.zeros((OUT, length), jnp.float32), (weight_parts, gated_parts))[0]
    return total.astype(jnp.bfloat16)
```

```python
import functools
import math

import jax
import jax.numpy as jnp
from jax import lax
from jax.experimental import pallas as pl
from jax.experimental.pallas import tpu as pltpu
from jax.sharding import PartitionSpec as P

GROUP_SIZE = 16
LANES = 128
BLOCK = 256
CHANNELS = 128
HALO_CHUNKS = 4
TOKEN_CHUNKS = 4


def shifted(value, axis, steps):
    count = lax.axis_size(axis)
    return lax.ppermute(value, axis, [(source, source + steps) for source in range(count - steps)])


def product_kernel(key_ref, value_ref, out_ref):
    product = key_ref[...].astype(jnp.float32) * value_ref[...].astype(jnp.float32)
    out_ref[...] = product.T.astype(jnp.bfloat16)


def product_chunk(key_input, value_input, first, rows):
    tokens_here = key_input.shape[0]
    start = first // CHANNELS
    spec = pl.BlockSpec((tokens_here, CHANNELS), lambda i: (0, start + i))
    return pl.pallas_call(
        product_kernel,
        grid=(rows // CHANNELS,),
        in_specs=[spec, spec],
        out_specs=pl.BlockSpec((CHANNELS, tokens_here), lambda i: (i, 0)),
        out_shape=jax.ShapeDtypeStruct((rows, tokens_here), jnp.bfloat16),
        cost_estimate=pl.CostEstimate(
            flops=rows * tokens_here, bytes_accessed=6 * rows * tokens_here, transcendentals=0
        ),
    )(key_input, value_input)


def conv_kernel(span, taps_length, with_alias, gate_ref, taps_ref, *refs):
    sources = refs[: span + 1]
    out_ref, gate_t, lines = refs[span + 1 + (1 if with_alias else 0) :]
    tokens_here = out_ref.shape[1]
    gate_t[...] = gate_ref[...].astype(jnp.float32).T
    lines[:, :taps_length] = taps_ref[...].astype(jnp.float32)
    lines[:, taps_length:] = jnp.zeros((lines.shape[0], LANES), jnp.float32)
    per_block = BLOCK // LANES
    lag_tiles = taps_length // LANES
    lag_blocks = lag_tiles + per_block
    out_blocks = tokens_here // BLOCK
    per_source = tokens_here // LANES
    first_tile = (span + 1) * per_source - per_source - lag_tiles
    zeros = jnp.zeros((LANES, LANES), jnp.bfloat16)

    def one_group(group):
        rows = pl.ds(pl.multiple_of(group * GROUP_SIZE, GROUP_SIZE), GROUP_SIZE)
        tiles = []
        for index in range(first_tile, (span + 1) * per_source):
            source, place = divmod(index, per_source)
            tiles.append(sources[source][rows, place * LANES : (place + 1) * LANES])
        signal = jnp.concatenate(
            [
                jnp.concatenate(
                    [tiles[block * per_block + lag] for block in range(out_blocks)], axis=0
                )
                for lag in range(lag_blocks)
            ],
            axis=1,
        )
        line = lines[pl.ds(group, 1), :]
        spread = jnp.broadcast_to(line, (LANES, line.shape[1]))
        band = pltpu.roll(spread, 0, 1, stride=1, stride_axis=0).astype(jnp.bfloat16)

        def tile(index):
            if index < 0 or index > lag_tiles:
                return zeros
            return band[:, index * LANES : (index + 1) * LANES]

        matrix = jnp.concatenate(
            [
                jnp.concatenate(
                    [tile(lag_tiles + across - lag) for across in range(per_block)], axis=1
                )
                for lag in range(lag_blocks)
            ],
            axis=0,
        )
        conv = jnp.dot(signal, matrix, preferred_element_type=jnp.float32)
        for block in range(out_blocks):
            part = conv[block * GROUP_SIZE : (block + 1) * GROUP_SIZE]
            columns = slice(block * BLOCK, (block + 1) * BLOCK)
            out_ref[rows, columns] = (gate_t[rows, columns] * part).astype(jnp.bfloat16)

    def pair(step, carry):
        one_group(2 * step)
        one_group(2 * step + 1)
        return carry

    lax.fori_loop(0, CHANNELS // GROUP_SIZE // 2, pair, 0)


def conv_chunk(gate_input, filter_taps, sources, gated, first):
    tokens_here, width = gate_input.shape
    rows = sources[0].shape[0]
    taps_length = filter_taps.shape[1]
    start = first // CHANNELS
    groups = CHANNELS // GROUP_SIZE
    span = len(sources) - 1
    in_specs = [
        pl.BlockSpec((tokens_here, CHANNELS), lambda i: (0, start + i)),
        pl.BlockSpec((groups, taps_length), lambda i: (start + i, 0)),
    ] + [pl.BlockSpec((CHANNELS, tokens_here), lambda i: (i, 0))] * (span + 1)
    operands = [gate_input, filter_taps, *sources]
    aliases = {}
    if gated is not None:
        in_specs.append(pl.BlockSpec(memory_space=pl.ANY))
        aliases = {len(operands): 0}
        operands.append(gated)
    return pl.pallas_call(
        functools.partial(conv_kernel, span, taps_length, gated is not None),
        grid=(rows // CHANNELS,),
        in_specs=in_specs,
        out_specs=pl.BlockSpec((CHANNELS, tokens_here), lambda i: (start + i, 0)),
        out_shape=jax.ShapeDtypeStruct((width, tokens_here), jnp.bfloat16),
        scratch_shapes=[
            pltpu.VMEM((CHANNELS, tokens_here), jnp.float32),
            pltpu.VMEM((groups, taps_length + LANES), jnp.float32),
        ],
        input_output_aliases=aliases,
        compiler_params=pltpu.CompilerParams(vmem_limit_bytes=40 * 1024 * 1024),
        cost_estimate=pl.CostEstimate(
            flops=4 * rows * tokens_here * taps_length,
            bytes_accessed=2 * rows * tokens_here * (span + 3),
            transcendentals=0,
        ),
    )(*operands)


def body(gate_input, key_input, value_input, filter_taps, out_weight):
    tokens_here, width = gate_input.shape
    span = -(-filter_taps.shape[1] // tokens_here)
    chunks = math.gcd(width // CHANNELS, HALO_CHUNKS)
    rows = width // chunks
    moved = []
    for chunk in range(chunks):
        own = product_chunk(key_input, value_input, chunk * rows, rows)
        moved.append([own])
    for chunk in range(chunks):
        for _ in range(span):
            moved[chunk].insert(0, shifted(moved[chunk][0], "seq", 1))
    gated = None
    for chunk in range(chunks):
        gated = conv_chunk(gate_input, filter_taps, moved[chunk], gated, chunk * rows)
    pieces = []
    step = tokens_here // TOKEN_CHUNKS
    for chunk in range(TOKEN_CHUNKS):
        partial = lax.dot_general(
            out_weight,
            gated[:, chunk * step : (chunk + 1) * step],
            (((1,), (0,)), ((), ())),
            preferred_element_type=jnp.float32,
        ).astype(jnp.bfloat16)
        pieces.append(lax.psum_scatter(partial, "tp", scatter_dimension=0, tiled=True))
    return jnp.concatenate(pieces, axis=1)


def solution(mesh):
    return jax.shard_map(
        body,
        mesh=mesh,
        in_specs=(P("seq", "tp"), P("seq", "tp"), P("seq", "tp"), P("tp", None), P(None, "tp")),
        out_specs=P("tp", "seq"),
        check_vma=False,
    )
```

```python
import functools
import math

import jax
import jax.numpy as jnp
from jax import lax
from jax.experimental import pallas as pl
from jax.experimental.pallas import tpu as pltpu
from jax.sharding import PartitionSpec as P

GROUP_SIZE = 16
LANES = 128
BLOCK = 256
CHANNELS = 128
HALO_CHUNKS = 4
TOKEN_CHUNKS = 4


def shifted(value, axis, steps):
    count = lax.axis_size(axis)
    return lax.ppermute(value, axis, [(source, source + steps) for source in range(count - steps)])


def product_kernel(key_ref, value_ref, out_ref):
    product = key_ref[...].astype(jnp.float32) * value_ref[...].astype(jnp.float32)
    out_ref[...] = product.T.astype(jnp.bfloat16)


def product_chunk(key_input, value_input, first, rows):
    tokens_here = key_input.shape[0]
    start = first // CHANNELS
    spec = pl.BlockSpec((tokens_here, CHANNELS), lambda i: (0, start + i))
    return pl.pallas_call(
        product_kernel,
        grid=(rows // CHANNELS,),
        in_specs=[spec, spec],
        out_specs=pl.BlockSpec((CHANNELS, tokens_here), lambda i: (i, 0)),
        out_shape=jax.ShapeDtypeStruct((rows, tokens_here), jnp.bfloat16),
        cost_estimate=pl.CostEstimate(
            flops=rows * tokens_here, bytes_accessed=6 * rows * tokens_here, transcendentals=0
        ),
    )(key_input, value_input)


def conv_kernel(span, taps_length, with_alias, gate_ref, taps_ref, *refs):
    sources = refs[: span + 1]
    out_ref, gate_t, lines = refs[span + 1 + (1 if with_alias else 0) :]
    tokens_here = out_ref.shape[1]
    gate_t[...] = gate_ref[...].astype(jnp.float32).T
    lines[:, :taps_length] = taps_ref[...].astype(jnp.float32)
    lines[:, taps_length:] = jnp.zeros((lines.shape[0], LANES), jnp.float32)
    per_block = BLOCK // LANES
    lag_tiles = taps_length // LANES
    lag_blocks = lag_tiles + per_block
    out_blocks = tokens_here // BLOCK
    per_source = tokens_here // LANES
    first_tile = (span + 1) * per_source - per_source - lag_tiles
    zeros = jnp.zeros((LANES, LANES), jnp.bfloat16)

    def one_group(group):
        rows = pl.ds(pl.multiple_of(group * GROUP_SIZE, GROUP_SIZE), GROUP_SIZE)
        tiles = []
        for index in range(first_tile, (span + 1) * per_source):
            source, place = divmod(index, per_source)
            tiles.append(sources[source][rows, place * LANES : (place + 1) * LANES])
        signal = jnp.concatenate(
            [
                jnp.concatenate(
                    [tiles[block * per_block + lag] for block in range(out_blocks)], axis=0
                )
                for lag in range(lag_blocks)
            ],
            axis=1,
        )
        line = lines[pl.ds(group, 1), :]
        spread = jnp.broadcast_to(line, (LANES, line.shape[1]))
        band = pltpu.roll(spread, 0, 1, stride=1, stride_axis=0).astype(jnp.bfloat16)

        def tile(index):
            if index < 0 or index > lag_tiles:
                return zeros
            return band[:, index * LANES : (index + 1) * LANES]

        matrix = jnp.concatenate(
            [
                jnp.concatenate(
                    [tile(lag_tiles + across - lag) for across in range(per_block)], axis=1
                )
                for lag in range(lag_blocks)
            ],
            axis=0,
        )
        conv = jnp.dot(signal, matrix, preferred_element_type=jnp.float32)
        for block in range(out_blocks):
            part = conv[block * GROUP_SIZE : (block + 1) * GROUP_SIZE]
            columns = slice(block * BLOCK, (block + 1) * BLOCK)
            out_ref[rows, columns] = (gate_t[rows, columns] * part).astype(jnp.bfloat16)

    def pair(step, carry):
        one_group(2 * step)
        one_group(2 * step + 1)
        return carry

    lax.fori_loop(0, CHANNELS // GROUP_SIZE // 2, pair, 0)


def conv_chunk(gate_input, filter_taps, sources, gated, first):
    tokens_here, width = gate_input.shape
    rows = sources[0].shape[0]
    taps_length = filter_taps.shape[1]
    start = first // CHANNELS
    groups = CHANNELS // GROUP_SIZE
    span = len(sources) - 1
    in_specs = [
        pl.BlockSpec((tokens_here, CHANNELS), lambda i: (0, start + i)),
        pl.BlockSpec((groups, taps_length), lambda i: (start + i, 0)),
    ] + [pl.BlockSpec((CHANNELS, tokens_here), lambda i: (i, 0))] * (span + 1)
    operands = [gate_input, filter_taps, *sources]
    aliases = {}
    if gated is not None:
        in_specs.append(pl.BlockSpec(memory_space=pl.ANY))
        aliases = {len(operands): 0}
        operands.append(gated)
    return pl.pallas_call(
        functools.partial(conv_kernel, span, taps_length, gated is not None),
        grid=(rows // CHANNELS,),
        in_specs=in_specs,
        out_specs=pl.BlockSpec((CHANNELS, tokens_here), lambda i: (start + i, 0)),
        out_shape=jax.ShapeDtypeStruct((width, tokens_here), jnp.bfloat16),
        scratch_shapes=[
            pltpu.VMEM((CHANNELS, tokens_here), jnp.float32),
            pltpu.VMEM((groups, taps_length + LANES), jnp.float32),
        ],
        input_output_aliases=aliases,
        compiler_params=pltpu.CompilerParams(vmem_limit_bytes=40 * 1024 * 1024),
        cost_estimate=pl.CostEstimate(
            flops=16 * rows * tokens_here * taps_length,
            bytes_accessed=2 * rows * tokens_here * (span + 3),
            transcendentals=0,
        ),
    )(*operands)


def first_parts(partial, axis):
    rows = partial.shape[0] // lax.axis_size(axis)
    return partial[-rows:], partial[:rows]


def scatter_sum(partial, ends, axis):
    count = lax.axis_size(axis)
    here = lax.axis_index(axis)
    rows = partial.shape[0] // count

    def part(index):
        start = jnp.clip(index, 0, count - 1) * rows
        return lax.dynamic_slice_in_dim(partial, start, rows, 0).astype(jnp.float32)

    upward = downward = None
    for step in range(1, count):
        if step == 1:
            up, down = ends
        else:
            up = part(count - step + here) + upward
            down = part(here - count + step) + downward
        upward = lax.ppermute(
            up.astype(jnp.bfloat16), axis, [(source, source + 1) for source in range(step)]
        ).astype(jnp.float32)
        downward = lax.ppermute(
            down.astype(jnp.bfloat16),
            axis,
            [(count - 1 - source, count - 2 - source) for source in range(step)],
        ).astype(jnp.float32)
    return (part(here) + upward + downward).astype(jnp.bfloat16)


def body(gate_input, key_input, value_input, filter_taps, out_weight):
    tokens_here, width = gate_input.shape
    span = -(-filter_taps.shape[1] // tokens_here)
    chunks = math.gcd(width // CHANNELS, HALO_CHUNKS)
    rows = width // chunks
    moved = []
    for chunk in range(chunks):
        own = product_chunk(key_input, value_input, chunk * rows, rows)
        moved.append([own])
    for chunk in range(chunks):
        moved[chunk].insert(0, shifted(moved[chunk][0], "seq", 1))
    gated = None
    for chunk in range(chunks):
        for later in range(chunks) if chunk == 0 else []:
            if later == chunks - 1 and later > 0:
                gated = conv_chunk(gate_input, filter_taps, moved[0], None, 0)
                moved[later][0], gated = lax.optimization_barrier((moved[later][0], gated))
            for _ in range(span - 1):
                moved[later].insert(0, shifted(moved[later][0], "seq", 1))
        if chunk > 0 or gated is None:
            gated = conv_chunk(gate_input, filter_taps, moved[chunk], gated, chunk * rows)
    pieces = []
    step = tokens_here // TOKEN_CHUNKS
    for chunk in range(TOKEN_CHUNKS):
        partial = lax.dot_general(
            out_weight,
            gated[:, chunk * step : (chunk + 1) * step],
            (((1,), (0,)), ((), ())),
            preferred_element_type=jnp.float32,
        ).astype(jnp.bfloat16)
        ends = first_parts(partial, "tp")
        gated, partial, ends = lax.optimization_barrier((gated, partial, ends))
        pieces.append(scatter_sum(partial, ends, "tp"))
    return jnp.concatenate(pieces, axis=1)


def solution(mesh):
    return jax.shard_map(
        body,
        mesh=mesh,
        in_specs=(P("seq", "tp"), P("seq", "tp"), P("seq", "tp"), P("tp", None), P(None, "tp")),
        out_specs=P("tp", "seq"),
        check_vma=False,
    )
```
